256 devices in a mesh: dp: 8 (over y, x_hi), mp: 32 (over x_lo, z, core).
Axes of the slice: x: 4 (x_hi: 2, x_lo: 2; x = x_hi * 2 + x_lo), y: 4, z: 8, core: 2. Of those that a mesh axis runs over, the one named last changes fastest.
Arguments:
- hidden: bfloat16 [2048, 28672], P(None, 'mp'), may hold values from -0.125 to 0.125
- grad_out: bfloat16 [2048, 16384], P('mp', 'dp'), may hold values from -6 to 6
- down_weight: bfloat16 [28672, 16384], P('mp', 'dp'), may hold values from -0.03125 to 0.03125
Outputs:
- grad_hidden: bfloat16 [2048, 28672], P('dp', 'mp')
- grad_weight: bfloat16 [28672, 16384], P('mp', 'dp')
The draws below stay inside these ranges and needn't reach their ends.
All inputs are finite; a program needn't handle non-finite values.
Results may differ from the reference program's by a relative error of at most 0.012.
Values may be sent and summed in bfloat16 or wider, within the bound.
No kernel may reach another device: no remote copies, remote signals or barrier semaphores. Data moves between devices by JAX's collectives and lax.ppermute only.
A program may use at most 64 MiB of HBM per device.

```python
import jax
import jax.numpy as jnp
from jax import lax

D = 16384
FF = 28672
TOKENS = 2048
N_DP = 8


def strengthened(array, stream_key, source, target, shards_of, factor):
    def block_of(position):
        return (jnp.arange(array.shape[position]) // (array.shape[position] // shards_of)).reshape((-1,) + (1,) * (array.ndim - 1 - position))

    one_side = jax.random.permutation(stream_key, shards_of)[block_of(target)]
    other_side = (block_of(target) + shards_of // 2) % shards_of
    return jnp.where((block_of(source) == one_side) | (block_of(source) == other_side), factor * array, array)


def steps_of(key, shape, split, least, high):
    factor_of, own = 1.0, jax.random.fold_in(key, 6)
    for position, shards_of in split:
        heights = jnp.exp(jax.random.uniform(jax.random.fold_in(own, position), (shards_of,), jnp.float32, least / len(split), high / len(split)))
        factor_of = factor_of * jnp.repeat(heights, shape[position] // shards_of).reshape([-1 if axis == position else 1 for axis in range(len(shape))])
    return factor_of


def centred(key, dims, width, limit, shards=(), held_as=jnp.bfloat16):
    drawn = jax.random.normal(key, dims, jnp.float32) * width
    if len(shards) > 0:
        drawn = steps_of(key, dims, shards, -0.22, 0.18) * drawn
    return jnp.clip(drawn, min=-limit, max=limit).astype(held_as)


def gaussian_with(stream_key, dims, deviation, limit, shards, heavy, held_as=jnp.bfloat16):
    drawn = deviation * jax.random.normal(stream_key, dims, jnp.float32)
    if shards:
        drawn = drawn * steps_of(stream_key, dims, shards, -0.22, 0.18)
    return jnp.clip(strengthened(drawn, jax.random.fold_in(stream_key, 3), *heavy), -limit, limit).astype(held_as)


def setup_inputs(seed: int = 0) -> dict:
    splits = jax.random.split(jax.random.key(seed), 4)
    return {
        "hidden": centred(splits[0], (TOKENS, FF), TOKENS ** -0.5, 0.125, ((1, 32),)),
        "grad_out": gaussian_with(splits[1], (TOKENS, D), 1.0, 6.0, ((0, 32), (1, 8)), (1, 0, 32, 2.75)),
        "down_weight": centred(splits[2], (FF, D), FF ** -0.5, 0.03125, ((0, 32), (1, 8))),
    }


def reference(hidden, grad_out, down_weight):
    slab_width = D // N_DP
    summed = jnp.zeros((TOKENS, FF), jnp.float32)
    for block_index in range(N_DP):
        grad_slab = grad_out[:, block_index * slab_width:(block_index + 1) * slab_width]
        weight_slab = down_weight[:, block_index * slab_width:(block_index + 1) * slab_width]
        partial_value = lax.dot_general(grad_slab, weight_slab, (((1,), (1,)), ((), ())), preferred_element_type=jnp.float32).astype(jnp.bfloat16)
        partial_value = lax.optimization_barrier(partial_value)
        summed = summed + partial_value.astype(jnp.float32)
    grad_weight = lax.dot_general(hidden, grad_out, (((0,), (0,)), ((), ())), preferred_element_type=jnp.float32)
    return summed.astype(jnp.bfloat16), grad_weight.astype(jnp.bfloat16)
```

```python
import jax
import jax.numpy as jnp
from jax import lax
from jax.experimental import pallas as pl
from jax.experimental.pallas import tpu as pltpu
from jax.sharding import PartitionSpec as P


AXES = ("dp", "mp")
NX, NY, NZ, NC = 4, 4, 8, 2
ROWS, WIDTH, UNITS, TOKENS = 64, 2048, 896, 2048
OWNED, HALF = 256, 128
MIB = 1 << 20


def flat(x, y, z, c):
    x, y, z = x % NX, y % NY, z % NZ
    return (y * 2 + x // 2) * 32 + (x % 2) * 16 + z * 2 + c


def pairs(move):
    return [
        (flat(x, y, z, c), flat(*move(x, y, z, c)))
        for x in range(NX) for y in range(NY) for z in range(NZ) for c in range(NC)
    ]


def send(value, move):
    return lax.ppermute(value, AXES, pairs(move))


def along_z(x, y, z, c):
    return (x, y, z + 1, c) if c == 0 else (x, y, z - 1, c)


def across_x(x, y, z, c):
    return (x ^ 1, y, z, c)


def other_core(x, y, z, c):
    return (x, y, z, 1 - c)


def along_y(d):
    return lambda x, y, z, c: (x, y + d, z, c)


def across_pairs(x, y, z, c):
    return (x ^ 2, y, z, c)


VMEM = pl.BlockSpec(memory_space=pltpu.VMEM)
HBM = pl.BlockSpec(memory_space=pl.ANY)


def place(pieces, panel=None):
    metas = [p[1:] for p in pieces]

    def body(*refs):
        blocks, out = refs[:len(pieces)], refs[-1]
        mp = lax.axis_index("mp")
        xlo, z, core = mp // 16, (mp // 2) % 8, mp % 2
        for ref, (flip_x, steps, flip_core, swapped) in zip(blocks, metas):
            lo = 1 - xlo if flip_x else xlo
            behind = core if swapped else 1 - core
            zz = (z + 8 + steps * (1 - 2 * behind)) % 8
            c = 1 - core if flip_core else core
            n = ref.shape[0]
            for half in range(n // ROWS):
                cc = c if half == 0 else 1 - c
                at = pl.multiple_of((lo * 16 + zz * 2 + cc) * ROWS, ROWS)
                out[pl.ds(at, ROWS), :] = ref[half * ROWS:(half + 1) * ROWS, :]

    args = [p[0] for p in pieces] + ([] if panel is None else [panel])
    return pl.pallas_call(
        body,
        out_shape=pltpu.VMEM((TOKENS, WIDTH), jnp.bfloat16),
        in_specs=[VMEM] * len(args),
        out_specs=VMEM,
        input_output_aliases={} if panel is None else {len(args) - 1: 0},
        compiler_params=pltpu.CompilerParams(vmem_limit_bytes=20 * MIB),
        cost_estimate=pl.CostEstimate(flops=0, bytes_accessed=2 * sum(p[0].size * 2 for p in pieces), transcendentals=0),
        name="place",
    )(*args)


def partials(panel, weight, outputs):
    shapes = [pltpu.VMEM((HALF * len(groups), UNITS), dtype) for dtype, groups in outputs]

    def body(panel_ref, w_ref, *outs):
        dp = lax.axis_index("dp")
        y, h = dp // 2, dp % 2
        for (dtype, groups), out in zip(outputs, outs):
            rows = []
            for dy, cross, half in groups:
                owner = ((y + dy) % NY) * 2 + (1 - h if cross else h)
                at = pl.multiple_of(owner * OWNED + half * HALF, HALF)
                rows.append(panel_ref[pl.ds(at, HALF), :])
            out[...] = lax.dot_general(
                jnp.concatenate(rows, 0), w_ref[...], (((1,), (1,)), ((), ())),
                preferred_element_type=jnp.float32,
            ).astype(dtype)

    total = sum(len(groups) for _, groups in outputs) * HALF
    return pl.pallas_call(
        body,
        out_shape=shapes,
        in_specs=[VMEM, VMEM],
        out_specs=[VMEM] * len(shapes),
        compiler_params=pltpu.CompilerParams(vmem_limit_bytes=20 * MIB),
        cost_estimate=pl.CostEstimate(
            flops=2 * total * UNITS * WIDTH, bytes_accessed=8 * MIB, transcendentals=0),
        name="partials",
    )(panel, weight)


def added(args, outputs):
    def body(*refs):
        for out, parts in zip(refs[len(args):], outputs):
            for k, terms in enumerate(parts):
                total = None
                for i, row in terms:
                    term = refs[i][row:row + HALF, :].astype(jnp.float32)
                    total = term if total is None else total + term
                out[k * HALF:(k + 1) * HALF, :] = total.astype(jnp.bfloat16)

    return pl.pallas_call(
        body,
        out_shape=[pltpu.VMEM((HALF * len(parts), UNITS), jnp.bfloat16) for parts in outputs],
        in_specs=[VMEM] * len(args),
        out_specs=[VMEM] * len(outputs),
        compiler_params=pltpu.CompilerParams(vmem_limit_bytes=16 * MIB),
        cost_estimate=pl.CostEstimate(flops=0, bytes_accessed=MIB, transcendentals=0),
        name="added",
    )(*args)


def transposed(hidden):
    def body(h_ref, out):
        for j in range(0, UNITS, 128):
            out[j:j + 128, :] = h_ref[:, j:j + 128].T

    return pl.pallas_call(
        body,
        out_shape=pltpu.VMEM((UNITS, TOKENS), jnp.bfloat16),
        in_specs=[VMEM],
        out_specs=VMEM,
        compiler_params=pltpu.CompilerParams(vmem_limit_bytes=20 * MIB),
        cost_estimate=pl.CostEstimate(flops=0, bytes_accessed=7 * MIB, transcendentals=0),
        name="transposed",
    )(hidden)


def weight_gradient(hidden_t, panel):
    cols = 512

    def body(h_ref, p_ref, out):
        out[...] = jnp.dot(h_ref[...], p_ref[...], preferred_element_type=jnp.float32).astype(jnp.bfloat16)

    return pl.pallas_call(
        body,
        grid=(WIDTH // cols,),
        out_shape=jax.ShapeDtypeStruct((UNITS, WIDTH), jnp.bfloat16),
        in_specs=[pl.BlockSpec((UNITS, TOKENS), lambda i: (0, 0)), pl.BlockSpec((TOKENS, cols), lambda i: (0, i))],
        out_specs=pl.BlockSpec((UNITS, cols), lambda i: (0, i)),
        compiler_params=pltpu.CompilerParams(vmem_limit_bytes=24 * MIB),
        cost_estimate=pl.CostEstimate(flops=2 * UNITS * WIDTH * TOKENS, bytes_accessed=16 * MIB, transcendentals=0),
        name="weight_gradient",
    )(hidden_t, panel)


def finished(own, swapped, near, far, crossed):
    def body(own_ref, swapped_ref, n0, n1, n2, f0, f1, f2, x_ref, out):
        def f32(ref, row):
            return ref[row:row + HALF, :].astype(jnp.float32)

        first = own_ref[:HALF, :] + f32(swapped_ref, HALF) + f32(f0, 0) + f32(f1, 0) + f32(f2, 0)
        out[:HALF, :] = first.astype(jnp.bfloat16)
        second = own_ref[HALF:, :] + f32(n0, 0) + f32(n1, 0) + f32(n2, 0) + f32(x_ref, 0)
        out[HALF:, :] = second.astype(jnp.bfloat16)

    return pl.pallas_call(
        body,
        out_shape=jax.ShapeDtypeStruct((OWNED, UNITS), jnp.bfloat16),
        in_specs=[VMEM] * 9,
        out_specs=VMEM,
        compiler_params=pltpu.CompilerParams(vmem_limit_bytes=16 * MIB),
        name="finished",
    )(own, swapped, *near, *far, crossed)


def layer(hidden, grad_out, down_weight):
    own = grad_out
    v = send(own, across_x)
    part = send(own, other_core)
    u = jnp.concatenate([own, part], 0)
    hidden_t = transposed(hidden)
    early = [(u, 0, 0, 0, 0), (v, 1, 0, 0, 0), (send(v, other_core), 1, 0, 1, 0)]
    late = []
    for s in range(1, 5):
        keep = early if s < 3 else late
        if s < 4:
            u = send(u, along_z)
            x = send(u[ROWS:], across_x)
            early += [(u, 0, s, 0, 0)]
            keep += [(send(u, other_core), 0, s, 1, 1)]
            keep += [(x, 1, s, 1, 0), (send(x, other_core), 1, s, 0, 1)]
        else:
            u = send(u[:ROWS], along_z)
            keep += [(u, 0, s, 0, 0), (send(u, other_core), 0, s, 1, 1)]
        v = send(v, along_z)
        keep += [(v, 1, s, 0, 0), (send(v, other_core), 1, s, 1, 1)]
    panel = place(early)
    panel = place(late, panel)

    A, B, HOME, AWAY = 0, 1, 0, 1
    f32, bf16 = jnp.float32, jnp.bfloat16

    def run(*outputs):
        return partials(panel, down_weight, outputs)

    def add(args, *outputs):
        return added(args, outputs)

    near = {}
    for d in (2, 1, 3):
        block, = run((bf16, [(d, HOME, B), (d, AWAY, B)]))
        near[d] = send(block, along_y(d))
        if d == 2:
            block, = run((bf16, [(1, AWAY, A), (3, AWAY, A)]))
            swap1 = send(block, across_pairs)
    block, = run((bf16, [(2, AWAY, A), (0, AWAY, A)]))
    swap2 = send(block, across_pairs)
    keep1, = run((f32, [(1, HOME, A), (3, HOME, A)]))
    block1, block3 = add([keep1, swap1], [[(0, 0), (1, 0)]], [[(0, HALF), (1, HALF)]])
    far = {1: send(block1, along_y(1)), 3: send(block3, along_y(3))}
    keep2, own = run((f32, [(2, HOME, A), (0, AWAY, B)]), (f32, [(0, HOME, A), (0, HOME, B)]))
    block, = add([keep2, swap2], [[(0, 0), (1, 0)]])
    far[2] = send(block, along_y(2))
    block, = add([keep2, near[1], near[2], near[3]], [[(0, HALF), (1, HALF), (2, HALF), (3, HALF)]])
    crossed = send(block, across_pairs)
    grad_weight = weight_gradient(hidden_t, panel)
    grad_hidden = finished(own, swap2, [near[d] for d in (1, 2, 3)], [far[d] for d in (1, 2, 3)], crossed)
    return (grad_hidden, grad_weight)


def solution(mesh):
    return jax.shard_map(
        layer,
        mesh=mesh,
        in_specs=(P(None, "mp"), P("mp", "dp"), P("mp", "dp")),
        out_specs=(P("dp", "mp"), P("mp", "dp")),
        check_vma=False,
    )
```

```python
import jax
import jax.numpy as jnp
from jax import lax
from jax.experimental import pallas as pl
from jax.experimental.pallas import tpu as pltpu
from jax.sharding import PartitionSpec as P


AXES = ("dp", "mp")
NX, NY, NZ, NC = 4, 4, 8, 2
ROWS, WIDTH, UNITS, TOKENS = 64, 2048, 896, 2048
OWNED, HALF = 256, 128
MIB = 1 << 20


def flat(x, y, z, c):
    x, y, z = x % NX, y % NY, z % NZ
    return (y * 2 + x // 2) * 32 + (x % 2) * 16 + z * 2 + c


def pairs(move):
    return [
        (flat(x, y, z, c), flat(*move(x, y, z, c)))
        for x in range(NX) for y in range(NY) for z in range(NZ) for c in range(NC)
    ]


def send(value, move):
    return lax.ppermute(value, AXES, pairs(move))


def forth(x, y, z, c):
    return (x, y, z + 1, c) if c == 0 else (x, y, z - 1, c)


def across_x(x, y, z, c):
    return (x ^ 1, y, z, c)


def other_core(x, y, z, c):
    return (x, y, z, 1 - c)


def along_y(d):
    return lambda x, y, z, c: (x, y + d, z, c)


def across_pairs(x, y, z, c):
    return (x ^ 2, y, z, c)


VMEM = pl.BlockSpec(memory_space=pltpu.VMEM)


SLOTS = (
    (0, 0), (1, 0), (0, 7), (0, 1), (0, 6), (0, 2), (1, 7), (1, 1),
    (0, 5), (0, 3), (0, 4), (1, 6), (1, 2), (1, 5), (1, 3), (1, 4),
)
BLOCK = 2 * ROWS
TILE = 512
EARLY = 8


def here():
    mp = lax.axis_index("mp")
    return mp // 16, (mp // 2) % NZ, mp % 2


def write(refs, metas, out):
    _, _, core = here()
    for ref, (flip, steps, other, relayed) in zip(refs, metas):
        behind = core if relayed else 1 - core
        ahead = SLOTS.index((flip, steps % NZ))
        slot = ahead + behind * (SLOTS.index((flip, -steps % NZ)) - ahead)
        c = 1 - core if other else core
        for half in range(ref.shape[0] // ROWS):
            at = pl.multiple_of(slot * BLOCK + (c if half == 0 else 1 - c) * ROWS, ROWS)
            out[pl.ds(at, ROWS), :] = ref[half * ROWS:(half + 1) * ROWS, :]


def place(pieces, panel):
    metas = [p[1:] for p in pieces]
    n = len(pieces)

    def body(*refs):
        write(refs[:n], metas, refs[-1])

    return pl.pallas_call(
        body,
        out_shape=pltpu.VMEM((TOKENS, WIDTH), jnp.bfloat16),
        in_specs=[VMEM] * (n + 1),
        out_specs=VMEM,
        input_output_aliases={n: 0},
        compiler_params=pltpu.CompilerParams(vmem_limit_bytes=20 * MIB),
        cost_estimate=pl.CostEstimate(flops=0, bytes_accessed=4 * MIB, transcendentals=0),
        name="place",
    )(*[p[0] for p in pieces], panel)


def stage(pieces, first, last, hidden_t, weight, state):
    metas = [p[1:] for p in pieces]
    n = len(pieces)

    def body(*refs):
        h_ref, panel, acc = refs[n], refs[-2], refs[-1]
        write(refs[:n], metas, panel)

        @pl.loop(0, WIDTH // TILE)
        def _(i):
            cols = pl.ds(pl.multiple_of(i * TILE, TILE), TILE)
            part = jnp.dot(
                h_ref[:, first * BLOCK:last * BLOCK], panel[first * BLOCK:last * BLOCK, cols],
                preferred_element_type=jnp.float32,
            )
            acc[:, cols] = part if state is None else acc[:, cols] + part

    extra = () if state is None else state
    return pl.pallas_call(
        body,
        out_shape=[pltpu.VMEM((TOKENS, WIDTH), jnp.bfloat16), pltpu.VMEM((UNITS, WIDTH), jnp.float32)],
        in_specs=[VMEM] * (n + 2 + len(extra)),
        out_specs=[VMEM, VMEM],
        input_output_aliases={n + 2 + k: k for k in range(len(extra))},
        compiler_params=pltpu.CompilerParams(vmem_limit_bytes=12 * MIB),
        cost_estimate=pl.CostEstimate(
            flops=2 * UNITS * WIDTH * (last - first) * BLOCK, bytes_accessed=14 * MIB, transcendentals=0),
        name="stage",
    )(*[p[0] for p in pieces], hidden_t, weight, *extra)


def partials(panel, weight, outputs):
    shapes = [pltpu.VMEM((HALF * len(groups), UNITS), dtype) for dtype, groups in outputs]

    def body(panel_ref, w_ref, *outs):
        dp = lax.axis_index("dp")
        y, h = dp // 2, dp % 2
        xlo, z, _ = here()
        for (dtype, groups), out in zip(outputs, outs):
            rows = []
            for dy, cross, half in groups:
                owner = ((y + dy) % NY) * 2 + (1 - h if cross else h)
                flip, dz = (owner // 4) ^ xlo, (2 * (owner % 4) + half - z + NZ) % NZ
                slot = sum(jnp.where((flip == f) & (dz == d), k, 0) for k, (f, d) in enumerate(SLOTS))
                at = pl.multiple_of(slot * BLOCK, BLOCK)
                rows.append(panel_ref[pl.ds(at, HALF), :])
            out[...] = lax.dot_general(
                jnp.concatenate(rows, 0), w_ref[...], (((1,), (1,)), ((), ())),
                preferred_element_type=jnp.float32,
            ).astype(dtype)

    total = sum(len(groups) for _, groups in outputs) * HALF
    return pl.pallas_call(
        body,
        out_shape=shapes,
        in_specs=[VMEM, VMEM],
        out_specs=[VMEM] * len(shapes),
        compiler_params=pltpu.CompilerParams(vmem_limit_bytes=20 * MIB),
        cost_estimate=pl.CostEstimate(
            flops=2 * total * UNITS * WIDTH, bytes_accessed=8 * MIB, transcendentals=0),
        name="partials",
    )(panel, weight)


def added(args, outputs):
    def body(*refs):
        for out, parts in zip(refs[len(args):], outputs):
            for k, terms in enumerate(parts):
                total = None
                for i, row in terms:
                    term = refs[i][row:row + HALF, :].astype(jnp.float32)
                    total = term if total is None else total + term
                out[k * HALF:(k + 1) * HALF, :] = total.astype(jnp.bfloat16)

    return pl.pallas_call(
        body,
        out_shape=[pltpu.VMEM((HALF * len(parts), UNITS), jnp.bfloat16) for parts in outputs],
        in_specs=[VMEM] * len(args),
        out_specs=[VMEM] * len(outputs),
        compiler_params=pltpu.CompilerParams(vmem_limit_bytes=16 * MIB),
        cost_estimate=pl.CostEstimate(flops=0, bytes_accessed=MIB, transcendentals=0),
        name="added",
    )(*args)


def transposed(hidden):
    def body(h_ref, out):
        xlo, z, _ = here()
        for k, (flip, dz) in enumerate(SLOTS):
            lo = 1 - xlo if flip else xlo
            at = pl.multiple_of((lo * 16 + (z + dz) % NZ * 2) * ROWS, BLOCK)
            out[:, k * BLOCK:(k + 1) * BLOCK] = h_ref[pl.ds(at, BLOCK), :].T

    return pl.pallas_call(
        body,
        out_shape=pltpu.VMEM((UNITS, TOKENS), jnp.bfloat16),
        in_specs=[VMEM],
        out_specs=VMEM,
        compiler_params=pltpu.CompilerParams(vmem_limit_bytes=12 * MIB),
        cost_estimate=pl.CostEstimate(flops=0, bytes_accessed=7 * MIB, transcendentals=0),
        name="transposed",
    )(hidden)


def weight_gradient(hidden_t, panel, acc):
    def body(h_ref, p_ref, acc_ref, out):
        late = jnp.dot(h_ref[:, EARLY * BLOCK:], p_ref[EARLY * BLOCK:, :], preferred_element_type=jnp.float32)
        out[...] = (acc_ref[...] + late).astype(jnp.bfloat16)

    return pl.pallas_call(
        body,
        grid=(WIDTH // TILE,),
        out_shape=jax.ShapeDtypeStruct((UNITS, WIDTH), jnp.bfloat16),
        in_specs=[
            pl.BlockSpec((UNITS, TOKENS), lambda i: (0, 0)),
            pl.BlockSpec((TOKENS, TILE), lambda i: (0, i)),
            pl.BlockSpec((UNITS, TILE), lambda i: (0, i)),
        ],
        out_specs=pl.BlockSpec((UNITS, TILE), lambda i: (0, i)),
        compiler_params=pltpu.CompilerParams(vmem_limit_bytes=24 * MIB),
        cost_estimate=pl.CostEstimate(
            flops=2 * UNITS * WIDTH * TOKENS, bytes_accessed=16 * MIB, transcendentals=0),
        name="weight_gradient",
    )(hidden_t, panel, acc)


def finished(own, swapped, near, far, crossed):
    def body(own_ref, swapped_ref, n0, n1, n2, f0, f1, f2, x_ref, out):
        def f32(ref, row):
            return ref[row:row + HALF, :].astype(jnp.float32)

        first = own_ref[:HALF, :] + f32(swapped_ref, HALF) + f32(f0, 0) + f32(f1, 0) + f32(f2, 0)
        out[:HALF, :] = first.astype(jnp.bfloat16)
        second = own_ref[HALF:, :] + f32(n0, 0) + f32(n1, 0) + f32(n2, 0) + f32(x_ref, 0)
        out[HALF:, :] = second.astype(jnp.bfloat16)

    return pl.pallas_call(
        body,
        out_shape=jax.ShapeDtypeStruct((OWNED, UNITS), jnp.bfloat16),
        in_specs=[VMEM] * 9,
        out_specs=VMEM,
        compiler_params=pltpu.CompilerParams(vmem_limit_bytes=16 * MIB),
        name="finished",
    )(own, swapped, *near, *far, crossed)


def layer(hidden, grad_out, down_weight):
    v = send(grad_out, across_x)
    part = send(grad_out, other_core)
    a, b = grad_out, part
    pieces = {
        0: [(a, 0, 0, 0, 0), (b, 0, 0, 1, 0), (v, 1, 0, 0, 0), (send(v, other_core), 1, 0, 1, 0)],
        1: [], 2: [], 3: [],
    }
    hidden_t = transposed(hidden)
    for s in range(1, 5):
        mine = pieces[min(s, 3)]
        across = pieces[min(s + 1, 3)]
        a = send(a, forth)
        v = send(v, forth)
        mine += [(a, 0, s, 0, 0)]
        across += [(v, 1, s, 0, 0), (send(v, other_core), 1, s, 1, 1)]
        if s < 4:
            b = send(b, forth)
            mine += [(b, 0, s, 1, 0), (send(jnp.concatenate([a, b], 0), other_core), 0, s, 1, 1)]
            x = send(b, across_x)
            across += [(x, 1, s, 1, 0), (send(x, other_core), 1, s, 0, 1)]
        else:
            mine += [(send(a, other_core), 0, s, 1, 1)]
    state = None
    for k, (first, last) in enumerate(((0, 2), (2, 4), (4, EARLY))):
        state = stage(pieces[k], first, last, hidden_t, down_weight, state)
    panel, acc = state
    panel = place(pieces[3], panel)

    A, B, HOME, AWAY = 0, 1, 0, 1
    f32, bf16 = jnp.float32, jnp.bfloat16

    def run(*outputs):
        return partials(panel, down_weight, outputs)

    def add(args, *outputs):
        return added(args, outputs)

    near = {}
    for d in (2, 1, 3):
        block, = run((bf16, [(d, HOME, B), (d, AWAY, B)]))
        near[d] = send(block, along_y(d))
        if d == 2:
            block, = run((bf16, [(1, AWAY, A), (3, AWAY, A)]))
            swap1 = send(block, across_pairs)
    block, = run((bf16, [(2, AWAY, A), (0, AWAY, A)]))
    swap2 = send(block, across_pairs)
    keep1, = run((f32, [(1, HOME, A), (3, HOME, A)]))
    block1, block3 = add([keep1, swap1], [[(0, 0), (1, 0)]], [[(0, HALF), (1, HALF)]])
    far = {1: send(block1, along_y(1)), 3: send(block3, along_y(3))}
    keep2, own = run((f32, [(2, HOME, A), (0, AWAY, B)]), (f32, [(0, HOME, A), (0, HOME, B)]))
    block, = add([keep2, swap2], [[(0, 0), (1, 0)]])
    far[2] = send(block, along_y(2))
    block, = add([keep2, near[1], near[2], near[3]], [[(0, HALF), (1, HALF), (2, HALF), (3, HALF)]])
    crossed = send(block, across_pairs)
    grad_weight = weight_gradient(hidden_t, panel, acc)
    grad_hidden = finished(own, swap2, [near[d] for d in (1, 2, 3)], [far[d] for d in (1, 2, 3)], crossed)
    return (grad_hidden, grad_weight)


def solution(mesh):
    return jax.shard_map(
        layer,
        mesh=mesh,
        in_specs=(P(None, "mp"), P("mp", "dp"), P("mp", "dp")),
        out_specs=(P("dp", "mp"), P("mp", "dp")),
        check_vma=False,
    )
```

```python
import jax
import jax.numpy as jnp
from jax import lax
from jax.experimental import pallas as pl
from jax.experimental.pallas import tpu as pltpu
from jax.sharding import PartitionSpec as P


AXES = ("dp", "mp")
NX, NY, NZ, NC = 4, 4, 8, 2
ROWS, WIDTH, UNITS, TOKENS = 64, 2048, 896, 2048
OWNED, HALF = 256, 128
MIB = 1 << 20


def flat(x, y, z, c):
    x, y, z = x % NX, y % NY, z % NZ
    return (y * 2 + x // 2) * 32 + (x % 2) * 16 + z * 2 + c


def pairs(move):
    return [
        (flat(x, y, z, c), flat(*move(x, y, z, c)))
        for x in range(NX) for y in range(NY) for z in range(NZ) for c in range(NC)
    ]


def send(value, move):
    return lax.ppermute(value, AXES, pairs(move))


def forth(x, y, z, c):
    return (x, y, z + 1, c) if c == 0 else (x, y, z - 1, c)


def across_x(x, y, z, c):
    return (x ^ 1, y, z, c)


def other_core(x, y, z, c):
    return (x, y, z, 1 - c)


def along_y(d):
    return lambda x, y, z, c: (x, y + d, z, c)


def across_pairs(x, y, z, c):
    return (x ^ 2, y, z, c)


VMEM = pl.BlockSpec(memory_space=pltpu.VMEM)


SLOTS = (
    (0, 0), (1, 0), (0, 7), (0, 1), (0, 6), (0, 2), (1, 7), (1, 1),
    (0, 5), (0, 3), (0, 4), (1, 6), (1, 2), (1, 5), (1, 3), (1, 4),
)
BLOCK = 2 * ROWS
TILE = 512
FIRST, EARLY = 4, 12


def here():
    mp = lax.axis_index("mp")
    return mp // 16, (mp // 2) % NZ, mp % 2


def write(refs, pieces, out):
    _, _, core = here()
    for i, row, flip, steps, other, relayed in pieces:
        behind = core if relayed else 1 - core
        ahead = SLOTS.index((flip, steps % NZ))
        slot = ahead + behind * (SLOTS.index((flip, -steps % NZ)) - ahead)
        c = 1 - core if other else core
        at = pl.multiple_of(slot * BLOCK + c * ROWS, ROWS)
        out[pl.ds(at, ROWS), :] = refs[i][row:row + ROWS, :]


def operands(pieces):
    blocks = []
    for p in pieces:
        if not any(p[0] is block for block in blocks):
            blocks.append(p[0])
    return blocks, [(next(i for i, b in enumerate(blocks) if b is p[0]),) + p[1:] for p in pieces]


def place(pieces, panel):
    blocks, pieces = operands(pieces)
    n = len(blocks)

    def body(*refs):
        write(refs[:n], pieces, refs[-1])

    return pl.pallas_call(
        body,
        out_shape=pltpu.VMEM((TOKENS, WIDTH), jnp.bfloat16),
        in_specs=[VMEM] * (n + 1),
        out_specs=VMEM,
        input_output_aliases={n: 0},
        compiler_params=pltpu.CompilerParams(vmem_limit_bytes=20 * MIB),
        cost_estimate=pl.CostEstimate(flops=0, bytes_accessed=4 * MIB, transcendentals=0),
        name="place",
    )(*blocks, panel)


def product(h_ref, panel, acc, first, last, start):
    @pl.loop(0, WIDTH // TILE)
    def _(i):
        cols = pl.ds(pl.multiple_of(i * TILE, TILE), TILE)
        part = jnp.dot(
            h_ref[:, first * BLOCK:last * BLOCK], panel[first * BLOCK:last * BLOCK, cols],
            preferred_element_type=jnp.float32,
        )
        acc[:, cols] = part if start else acc[:, cols] + part


def begin(pieces, hidden_t, weight):
    blocks, pieces = operands(pieces)
    n = len(blocks)

    def body(*refs):
        write(refs[:n], pieces, refs[-2])
        product(refs[n], refs[-2], refs[-1], 0, FIRST, True)

    return pl.pallas_call(
        body,
        out_shape=[pltpu.VMEM((TOKENS, WIDTH), jnp.bfloat16), pltpu.VMEM((UNITS, WIDTH), jnp.float32)],
        in_specs=[VMEM] * (n + 2),
        out_specs=[VMEM, VMEM],
        compiler_params=pltpu.CompilerParams(vmem_limit_bytes=12 * MIB),
        cost_estimate=pl.CostEstimate(
            flops=2 * UNITS * WIDTH * FIRST * BLOCK, bytes_accessed=14 * MIB, transcendentals=0),
        name="begin",
    )(*blocks, hidden_t, weight)


def accumulate(hidden_t, panel, acc):
    def body(h_ref, p_ref, _, out):
        product(h_ref, p_ref, out, FIRST, EARLY, False)

    return pl.pallas_call(
        body,
        out_shape=pltpu.VMEM((UNITS, WIDTH), jnp.float32),
        in_specs=[VMEM] * 3,
        out_specs=VMEM,
        input_output_aliases={2: 0},
        compiler_params=pltpu.CompilerParams(vmem_limit_bytes=12 * MIB),
        cost_estimate=pl.CostEstimate(
            flops=2 * UNITS * WIDTH * (EARLY - FIRST) * BLOCK, bytes_accessed=14 * MIB, transcendentals=0),
        name="accumulate",
    )(hidden_t, panel, acc)


def partials(panel, weight, outputs):
    shapes = [pltpu.VMEM((HALF * len(groups), UNITS), dtype) for dtype, groups in outputs]

    def body(panel_ref, w_ref, *outs):
        dp = lax.axis_index("dp")
        y, h = dp // 2, dp % 2
        xlo, z, _ = here()
        for (dtype, groups), out in zip(outputs, outs):
            rows = []
            for dy, cross, half in groups:
                owner = ((y + dy) % NY) * 2 + (1 - h if cross else h)
                flip, dz = (owner // 4) ^ xlo, (2 * (owner % 4) + half - z + NZ) % NZ
                slot = sum(jnp.where((flip == f) & (dz == d), k, 0) for k, (f, d) in enumerate(SLOTS))
                at = pl.multiple_of(slot * BLOCK, BLOCK)
                rows.append(panel_ref[pl.ds(at, HALF), :])
            out[...] = lax.dot_general(
                jnp.concatenate(rows, 0), w_ref[...], (((1,), (1,)), ((), ())),
                preferred_element_type=jnp.float32,
            ).astype(dtype)

    total = sum(len(groups) for _, groups in outputs) * HALF
    return pl.pallas_call(
        body,
        out_shape=shapes,
        in_specs=[VMEM, VMEM],
        out_specs=[VMEM] * len(shapes),
        compiler_params=pltpu.CompilerParams(vmem_limit_bytes=20 * MIB),
        cost_estimate=pl.CostEstimate(
            flops=2 * total * UNITS * WIDTH, bytes_accessed=8 * MIB, transcendentals=0),
        name="partials",
    )(panel, weight)


def added(args, outputs):
    def body(*refs):
        for out, parts in zip(refs[len(args):], outputs):
            for k, terms in enumerate(parts):
                total = None
                for i, row in terms:
                    term = refs[i][row:row + HALF, :].astype(jnp.float32)
                    total = term if total is None else total + term
                out[k * HALF:(k + 1) * HALF, :] = total.astype(jnp.bfloat16)

    return pl.pallas_call(
        body,
        out_shape=[pltpu.VMEM((HALF * len(parts), UNITS), jnp.bfloat16) for parts in outputs],
        in_specs=[VMEM] * len(args),
        out_specs=[VMEM] * len(outputs),
        compiler_params=pltpu.CompilerParams(vmem_limit_bytes=16 * MIB),
        cost_estimate=pl.CostEstimate(flops=0, bytes_accessed=MIB, transcendentals=0),
        name="added",
    )(*args)


def transposed(hidden):
    def body(h_ref, out):
        xlo, z, _ = here()
        for k, (flip, dz) in enumerate(SLOTS):
            lo = 1 - xlo if flip else xlo
            at = pl.multiple_of((lo * 16 + (z + dz) % NZ * 2) * ROWS, BLOCK)
            out[:, k * BLOCK:(k + 1) * BLOCK] = h_ref[pl.ds(at, BLOCK), :].T

    return pl.pallas_call(
        body,
        out_shape=pltpu.VMEM((UNITS, TOKENS), jnp.bfloat16),
        in_specs=[VMEM],
        out_specs=VMEM,
        compiler_params=pltpu.CompilerParams(vmem_limit_bytes=12 * MIB),
        cost_estimate=pl.CostEstimate(flops=0, bytes_accessed=7 * MIB, transcendentals=0),
        name="transposed",
    )(hidden)


def weight_gradient(hidden_t, panel, acc):
    def body(h_ref, p_ref, acc_ref, out):
        late = jnp.dot(h_ref[:, EARLY * BLOCK:], p_ref[EARLY * BLOCK:, :], preferred_element_type=jnp.float32)
        out[...] = (acc_ref[...] + late).astype(jnp.bfloat16)

    return pl.pallas_call(
        body,
        grid=(WIDTH // TILE,),
        out_shape=jax.ShapeDtypeStruct((UNITS, WIDTH), jnp.bfloat16),
        in_specs=[
            pl.BlockSpec((UNITS, TOKENS), lambda i: (0, 0)),
            pl.BlockSpec((TOKENS, TILE), lambda i: (0, i)),
            pl.BlockSpec((UNITS, TILE), lambda i: (0, i)),
        ],
        out_specs=pl.BlockSpec((UNITS, TILE), lambda i: (0, i)),
        compiler_params=pltpu.CompilerParams(vmem_limit_bytes=24 * MIB),
        cost_estimate=pl.CostEstimate(
            flops=2 * UNITS * WIDTH * TOKENS, bytes_accessed=16 * MIB, transcendentals=0),
        name="weight_gradient",
    )(hidden_t, panel, acc)


def finished(own, swapped, near, far, crossed):
    def body(own_ref, swapped_ref, n0, n1, n2, f0, f1, f2, x_ref, out):
        def f32(ref, row):
            return ref[row:row + HALF, :].astype(jnp.float32)

        first = own_ref[:HALF, :] + f32(swapped_ref, HALF) + f32(f0, 0) + f32(f1, 0) + f32(f2, 0)
        out[:HALF, :] = first.astype(jnp.bfloat16)
        second = own_ref[HALF:, :] + f32(n0, 0) + f32(n1, 0) + f32(n2, 0) + f32(x_ref, 0)
        out[HALF:, :] = second.astype(jnp.bfloat16)

    return pl.pallas_call(
        body,
        out_shape=jax.ShapeDtypeStruct((OWNED, UNITS), jnp.bfloat16),
        in_specs=[VMEM] * 9,
        out_specs=VMEM,
        compiler_params=pltpu.CompilerParams(vmem_limit_bytes=16 * MIB),
        name="finished",
    )(own, swapped, *near, *far, crossed)


def layer(hidden, grad_out, down_weight):
    part = send(grad_out, other_core)
    a, b, v, x = {0: grad_out}, {0: part}, {0: send(grad_out, across_x)}, {}
    for s in range(1, 5):
        a[s] = send(a[s - 1], forth)
        v[s] = send(v[s - 1], forth)
        if s < 4:
            b[s] = send(b[s - 1], forth)
            x[s] = send(b[s], across_x)
    hidden_t = transposed(hidden)

    def swapped(*streams):
        kinds = {"a": (a, 0, 0), "b": (b, 0, 1), "v": (v, 1, 0), "x": (x, 1, 1)}
        blocks = [kinds[k][0][s] for k, s in streams]
        moved = send(jnp.concatenate(blocks, 0), other_core)
        result = []
        for i, (k, s) in enumerate(streams):
            _, flip, other = kinds[k]
            result += [(blocks[i], 0, flip, s, other, 0), (moved, i * ROWS, flip, s, 1 - other, 1)]
        return result

    first = [(grad_out, 0, 0, 0, 0, 0), (part, 0, 0, 0, 1, 0)] + swapped(("v", 0), ("a", 1), ("b", 1))
    rest = swapped(("a", 2), ("b", 2), ("v", 1), ("x", 1)) + swapped(("a", 3), ("b", 3), ("v", 2), ("x", 2))
    rest += swapped(("v", 3), ("a", 4)) + swapped(("v", 4), ("x", 3))
    panel, acc = begin(first, hidden_t, down_weight)
    panel = place(rest, panel)

    A, B, HOME, AWAY = 0, 1, 0, 1
    f32, bf16 = jnp.float32, jnp.bfloat16

    def run(*outputs):
        return partials(panel, down_weight, outputs)

    def add(args, *outputs):
        return added(args, outputs)

    near = {}
    for d in (2, 1, 3):
        block, = run((bf16, [(d, HOME, B), (d, AWAY, B)]))
        near[d] = send(block, along_y(d))
        if d == 2:
            block, = run((bf16, [(1, AWAY, A), (3, AWAY, A)]))
            swap1 = send(block, across_pairs)
    block, = run((bf16, [(2, AWAY, A), (0, AWAY, A)]))
    swap2 = send(block, across_pairs)
    keep1, = run((f32, [(1, HOME, A), (3, HOME, A)]))
    block1, block3 = add([keep1, swap1], [[(0, 0), (1, 0)]], [[(0, HALF), (1, HALF)]])
    far = {1: send(block1, along_y(1)), 3: send(block3, along_y(3))}
    keep2, own = run((f32, [(2, HOME, A), (0, AWAY, B)]), (f32, [(0, HOME, A), (0, HOME, B)]))
    acc = accumulate(hidden_t, panel, acc)
    block, = add([keep2, swap2], [[(0, 0), (1, 0)]])
    far[2] = send(block, along_y(2))
    block, = add([keep2, near[1], near[2], near[3]], [[(0, HALF), (1, HALF), (2, HALF), (3, HALF)]])
    crossed = send(block, across_pairs)
    grad_weight = weight_gradient(hidden_t, panel, acc)
    grad_hidden = finished(own, swap2, [near[d] for d in (1, 2, 3)], [far[d] for d in (1, 2, 3)], crossed)
    return (grad_hidden, grad_weight)


def solution(mesh):
    return jax.shard_map(
        layer,
        mesh=mesh,
        in_specs=(P(None, "mp"), P("mp", "dp"), P("mp", "dp")),
        out_specs=(P("dp", "mp"), P("mp", "dp")),
        check_vma=False,
    )
```
